32 devices in a mesh: seq: 16 (over z, x, core), head: 2 (over y).
Axes of the slice: x: 2, y: 2, z: 4, core: 2. Of those that a mesh axis runs over, the one named last changes fastest.
Arguments:
- queries: bfloat16 [1, 4096, 8192], P(None, ('seq', 'head')), may hold values from -38 to 38
- keys: bfloat16 [1, 4096, 1024], P(None, ('seq', 'head')), may hold values from -6 to 6
- values: bfloat16 [1, 4096, 1024], P(None, ('seq', 'head')), may hold values from -6 to 6
- output_gradient: bfloat16 [1, 4096, 8192], P(None, ('seq', 'head')), may hold values from -6 to 6
- kv_blocks: int32 [32, 8], replicated, may hold values from -1 to 31, as said below
- block_position: int32 [32], replicated, may hold values from 0 to 31, as said below
Outputs:
- attention: bfloat16 [1, 4096, 8192], P(None, 'seq', 'head')
- query_grad: bfloat16 [1, 4096, 8192], P(None, 'seq', 'head')
- key_gradient: bfloat16 [1, 4096, 1024], P(None, 'seq', 'head')
- value_gradient: bfloat16 [1, 4096, 1024], P(None, 'seq', 'head')
The draws below stay inside these ranges and needn't reach their ends.
Inputs may be any that keep to these rules, and one draw needn't show every extreme that they name: `block_position`: stored blocks 2d and 2d + 1 hold logical blocks k and 31 - k, for one k per d and each k once. `kv_blocks`: row p lists p, then p - 1 (-1 if p = 0), then each global block g < 2 if g < p - 1 (else -1), then up to 4 distinct blocks from 2 to p - 2 (-1 for missing ones). For logical blocks k and 31 - k together, the listed blocks of 2 or more that lie outside that pair lie in distinct pairs k2, 31 - k2, and each is listed once.
All inputs are finite; a program needn't handle non-finite values.
Results may differ from the reference program's by a relative error of at most 0.03.
Values may be sent and summed in bfloat16 or wider, within the bound.
No kernel may reach another device: no remote copies, remote signals or barrier semaphores. Data moves between devices by JAX's collectives and lax.ppermute only.
A program may use at most 192 MiB of HBM per device.

```python
import jax
import jax.numpy as jnp
from jax import lax

QUERY_HEADS = 64
KEY_VALUE_HEADS = 8
HEAD_SIZE = 128
SEQUENCE_COUNT = 1
BLOCK_TOKENS = 128
WIN = 2
GLOB = 2
RAND = 4
BLOCKS_PER_SEQ = 32
SEQUENCE_LENGTH = 4096


def draw_block_position(key, part):
    pair_total = BLOCKS_PER_SEQ // 2
    order = jax.random.permutation(key, pair_total).astype(jnp.int32)
    stacked = jnp.stack([order, BLOCKS_PER_SEQ - 1 - order], axis=1)
    return stacked.reshape(BLOCKS_PER_SEQ).astype(jnp.int32)


def block_rows(row_blocks, picked):
    window = [jnp.where(row_blocks - offset >= 0, row_blocks - offset, -1) for offset in range(WIN)]
    globals_listed = [jnp.where(glob_number < row_blocks - WIN + 1, glob_number, -1) * jnp.ones_like(row_blocks) for glob_number in range(GLOB)]
    return jnp.concatenate(window + globals_listed + [picked], axis=1).astype(jnp.int32)


def draw_kv_blocks(key, part):
    pair_total = BLOCKS_PER_SEQ // 2
    pair_index = jnp.arange(pair_total, dtype=jnp.int32)[:, None]
    candidate = jnp.arange(pair_total, dtype=jnp.int32)[None, :]
    random_rank = jax.random.randint(key, (pair_total, pair_total), 0, 32768, dtype=jnp.int32)
    ranking = random_rank * pair_total + candidate
    usable = (candidate >= GLOB) & (jnp.abs(candidate - pair_index) > WIN - 1)
    early_rank = jnp.where(usable & (candidate < pair_index), ranking, -1)
    early_top = lax.top_k(early_rank, RAND)[0]
    early_pick = jnp.where(early_top >= 0, early_top % pair_total, -1)
    taken = jnp.any(candidate[:, :, None] == early_pick[:, None, :], axis=2)
    late_rank = jnp.where(usable & ~taken, ranking, -1)
    late_top = lax.top_k(late_rank, RAND)[0]
    late_pair = late_top % pair_total
    late_block = jnp.where(late_pair > pair_index, BLOCKS_PER_SEQ - 1 - late_pair, late_pair)
    late_pick = jnp.where(late_top >= 0, late_block, -1)
    early_rows = block_rows(pair_index, early_pick)
    late_rows = block_rows(BLOCKS_PER_SEQ - 1 - pair_index, late_pick)
    return jnp.concatenate([early_rows, late_rows[::-1]], axis=0).astype(jnp.int32)


def draw_keys(key, part):
    final_output = jnp.clip(jax.random.normal(jax.random.fold_in(key, 3), (SEQUENCE_COUNT, SEQUENCE_LENGTH, KEY_VALUE_HEADS * HEAD_SIZE), jnp.float32), -6.0, 6.0)
    return final_output.astype(jnp.bfloat16)


def draw_queries(key, part):
    final_output = jnp.clip(jax.random.normal(jax.random.fold_in(key, 5), (SEQUENCE_COUNT, SEQUENCE_LENGTH, QUERY_HEADS * HEAD_SIZE), jnp.float32), -6.0, 6.0)
    return final_output.astype(jnp.bfloat16)


def shard_levels(own_key, shape, cuts, smallest, largest):
    def one(axis_at, shards_of):
        steps = jax.random.uniform(jax.random.fold_in(jax.random.fold_in(own_key, 6), axis_at), (shards_of,), jnp.float32, smallest / len(cuts), largest / len(cuts))
        return jnp.repeat(jnp.exp(steps), shape[axis_at] // shards_of).reshape((-1,) + (1,) * (len(shape) - axis_at - 1))

    gain = one(*cuts[0])
    for cut in cuts[1:]:
        gain = gain * one(*cut)
    return gain


def noise(key, extent, width, bound, shards=(), kind=jnp.bfloat16):
    result = jax.random.normal(key, extent, jnp.float32) * width
    if len(shards) > 0:
        result = shard_levels(key, extent, shards, -0.22, 0.18) * result
    return jnp.clip(result, min=-bound, max=bound).astype(kind)


def setup_inputs(seed: int = 0) -> dict:
    streams_of = jax.random.split(jax.random.key(seed), 7)
    return {
        "queries": draw_queries(jax.random.fold_in(streams_of[6], 71), 0),
        "keys": draw_keys(jax.random.fold_in(streams_of[6], 71), 0),
        "values": noise(streams_of[2], (SEQUENCE_COUNT, SEQUENCE_LENGTH, KEY_VALUE_HEADS * HEAD_SIZE), 1.0, 6.0, ((1, 32),)),
        "output_gradient": noise(streams_of[3], (SEQUENCE_COUNT, SEQUENCE_LENGTH, QUERY_HEADS * HEAD_SIZE), 1.0, 6.0, ((1, 32),)),
        "kv_blocks": draw_kv_blocks(jax.random.fold_in(streams_of[6], 71), 0),
        "block_position": draw_block_position(jax.random.fold_in(streams_of[6], 71), 0),
    }


def stored_index(block_position):
    block_list = block_position.shape[0]
    stored = jnp.arange(block_list, dtype=jnp.int32)
    matches = block_position[None, :] == stored[:, None]
    return jnp.sum(jnp.where(matches, stored[None, :], 0), axis=1).astype(jnp.int32)


def reference(queries, keys, values, output_gradient, kv_blocks, block_position):
    sequence_list = queries.shape[0]
    block_list = block_position.shape[0]
    slot_number = kv_blocks.shape[1]
    group_view = QUERY_HEADS // KEY_VALUE_HEADS
    factor = HEAD_SIZE ** -0.5
    located = stored_index(block_position)
    query_array = queries.reshape(sequence_list, block_list, BLOCK_TOKENS, KEY_VALUE_HEADS, group_view, HEAD_SIZE)
    gradient_array = output_gradient.reshape(sequence_list, block_list, BLOCK_TOKENS, KEY_VALUE_HEADS, group_view, HEAD_SIZE)
    key_array = keys.reshape(sequence_list, block_list, BLOCK_TOKENS, KEY_VALUE_HEADS, HEAD_SIZE)
    value_array = values.reshape(sequence_list, block_list, BLOCK_TOKENS, KEY_VALUE_HEADS, HEAD_SIZE)
    positions = jnp.arange(BLOCK_TOKENS, dtype=jnp.int32)
    causal = positions[None, :] <= positions[:, None]

    def one_pair(carry, pair_number):
        key_sum_total, value_sum_total = carry
        first = pair_number * 2
        logical = lax.dynamic_slice_in_dim(block_position, first, 2)
        listed = jnp.take(kv_blocks, logical, axis=0)
        present = listed >= 0
        named = jnp.maximum(listed, 0)
        owner_devices = jnp.take(located, named.reshape(-1)).astype(jnp.int32)
        query_pair = lax.dynamic_slice_in_dim(query_array, first, 2, 1).astype(jnp.float32)
        grad_pair = lax.dynamic_slice_in_dim(gradient_array, first, 2, 1).astype(jnp.float32)
        key_block_set = jnp.take(key_array, owner_devices, axis=1).reshape(sequence_list, 2, slot_number, BLOCK_TOKENS, KEY_VALUE_HEADS, HEAD_SIZE).astype(jnp.float32)
        value_block_set = jnp.take(value_array, owner_devices, axis=1).reshape(sequence_list, 2, slot_number, BLOCK_TOKENS, KEY_VALUE_HEADS, HEAD_SIZE).astype(jnp.float32)
        itself = listed == logical[:, None]
        allowed = present[:, :, None, None] & (~itself[:, :, None, None] | causal[None, None])
        scores = jnp.einsum('scikgd,scejkd->sckgeij', query_pair, key_block_set) * factor
        scores = jnp.where(allowed[None, :, None, None], scores, -jnp.inf)
        highest = jnp.max(scores, axis=(4, 6), keepdims=True)
        totals = jnp.sum(jnp.exp(scores - highest), axis=(4, 6), keepdims=True)
        log_total = highest + jnp.log(totals)
        probs = jnp.exp(scores - log_total)
        probs_half = lax.optimization_barrier(probs.astype(jnp.bfloat16)).astype(jnp.float32)
        attention = jnp.einsum('sckgeij,scejkd->scikgd', probs_half, value_block_set).astype(jnp.bfloat16)
        attention_wide = lax.optimization_barrier(attention).astype(jnp.float32)
        delta = jnp.sum(grad_pair * attention_wide, axis=-1)
        dprobs = jnp.einsum('scikgd,scejkd->sckgeij', grad_pair, value_block_set)
        spread = jnp.moveaxis(delta, 2, 4)[:, :, :, :, None, :, None]
        dscores = lax.optimization_barrier((probs * (dprobs - spread) * factor).astype(jnp.bfloat16)).astype(jnp.float32)
        query_grad = jnp.einsum('sckgeij,scejkd->scikgd', dscores, key_block_set).astype(jnp.bfloat16)
        key_pieces = jnp.einsum('sckgeij,scikgd->scejkd', dscores, query_pair)
        value_pieces = jnp.einsum('sckgeij,scikgd->scejkd', probs_half, grad_pair)
        foreign = owner_devices.reshape(2, slot_number) // 2 != pair_number
        rounded = (present & (listed >= GLOB) & foreign)[None, :, :, None, None, None]
        key_pieces = jnp.where(rounded, lax.optimization_barrier(key_pieces.astype(jnp.bfloat16)).astype(jnp.float32), key_pieces)
        value_pieces = jnp.where(rounded, lax.optimization_barrier(value_pieces.astype(jnp.bfloat16)).astype(jnp.float32), value_pieces)
        active_mask = present[None, :, :, None, None, None]
        key_pieces = jnp.where(active_mask, key_pieces, 0.0).reshape(sequence_list, 2 * slot_number, BLOCK_TOKENS, KEY_VALUE_HEADS, HEAD_SIZE)
        value_pieces = jnp.where(active_mask, value_pieces, 0.0).reshape(sequence_list, 2 * slot_number, BLOCK_TOKENS, KEY_VALUE_HEADS, HEAD_SIZE)
        key_sum_total = key_sum_total.at[:, owner_devices].add(key_pieces)
        value_sum_total = value_sum_total.at[:, owner_devices].add(value_pieces)
        return (key_sum_total, value_sum_total), (attention, query_grad)

    zeroed_array = jnp.zeros((sequence_list, block_list, BLOCK_TOKENS, KEY_VALUE_HEADS, HEAD_SIZE), jnp.float32)
    pair_numbers = jnp.arange(block_list // 2, dtype=jnp.int32)
    (key_sum_total, value_sum_total), (attention, query_grad) = lax.scan(one_pair, (zeroed_array, zeroed_array), pair_numbers)

    def restore(stacked):
        return jnp.moveaxis(stacked, 0, 1).reshape(sequence_list, block_list * BLOCK_TOKENS, QUERY_HEADS * HEAD_SIZE)

    key_gradient = key_sum_total.reshape(sequence_list, block_list * BLOCK_TOKENS, KEY_VALUE_HEADS * HEAD_SIZE).astype(jnp.bfloat16)
    value_gradient = value_sum_total.reshape(sequence_list, block_list * BLOCK_TOKENS, KEY_VALUE_HEADS * HEAD_SIZE).astype(jnp.bfloat16)
    return (restore(attention), restore(query_grad), key_gradient, value_gradient)
```

```python
import functools

import jax
import jax.numpy as jnp
from jax import lax
from jax.experimental import pallas as pl
from jax.experimental.pallas import tpu as pltpu
from jax.sharding import PartitionSpec as P

QUERY_HEADS = 64
KEY_VALUE_HEADS = 8
HEAD_SIZE = 128
BLOCK_TOKENS = 128
GLOB = 2
GROUP = QUERY_HEADS // KEY_VALUE_HEADS
GROUP_WIDTH = GROUP * HEAD_SIZE
HEADS_AT_ONCE = 4
LOG2E = 1.4426950408889634
FACTOR = HEAD_SIZE ** (-0.5)


NT = (((1,), (1,)), ((), ()))
TN = (((0,), (0,)), ((), ()))
NN = (((1,), (0,)), ((), ()))


def dot(a, b, dims):
    return lax.dot_general(a, b, dims, preferred_element_type=jnp.float32)


def stored_index(block_position):
    block_list = block_position.shape[0]
    stored = jnp.arange(block_list, dtype=jnp.int32)
    matches = block_position[None, :] == stored[:, None]
    return jnp.sum(jnp.where(matches, stored[None, :], 0), axis=1)


def attend_block(i, slot_ref, q_ref, g_ref, kv_ref, a_ref, dq_ref, total, keys_at, values_at, part, slots):
    b = BLOCK_TOKENS
    d = HEAD_SIZE
    rows = HEADS_AT_ONCE * b
    for e in range(slots):
        at = jnp.maximum(slot_ref[i * slots + e], 0)
        keys_at[e * b : (e + 1) * b, :] = kv_ref[at, :, :d]
        values_at[e * b : (e + 1) * b, :] = kv_ref[at, :, d:]
    bias = [
        jnp.where(slot_ref[i * slots + e] >= 0, 0.0, jnp.inf).astype(jnp.float32) for e in range(slots)
    ]
    part[...] = jnp.zeros_like(part)

    def heads(j, carry):
        spans = [pl.ds((j * HEADS_AT_ONCE + t) * d, d) for t in range(HEADS_AT_ONCE)]
        q = jnp.concatenate([q_ref[i, :, span] for span in spans], axis=0)
        g = jnp.concatenate([g_ref[i, :, span] for span in spans], axis=0)
        k = keys_at[...]
        v = values_at[...]
        s = dot(q, k, NT)
        column = lax.broadcasted_iota(jnp.int32, (rows, b), 1)
        row = lax.broadcasted_iota(jnp.int32, (rows, b), 0) & (b - 1)
        tiles = [jnp.where(column <= row, s[:, :b], -jnp.inf)]
        tiles += [s[:, e * b : (e + 1) * b] for e in range(1, slots)]
        high = tiles[0]
        for e in range(1, slots):
            high = jnp.maximum(high, tiles[e] - bias[e])
        high = jnp.max(high, axis=1, keepdims=True) * (FACTOR * LOG2E)
        powers = [jnp.exp2(tiles[e] * (FACTOR * LOG2E) - (high + bias[e])) for e in range(slots)]
        inverse = 1.0 / jnp.sum(functools.reduce(jnp.add, powers), axis=1, keepdims=True)
        probs = jnp.concatenate([power * inverse for power in powers], axis=1)
        probs_half = probs.astype(jnp.bfloat16)
        out = dot(probs_half, v, NN).astype(jnp.bfloat16)
        dprobs = dot(g, v, NT)
        delta = jnp.sum(g.astype(jnp.float32) * out.astype(jnp.float32), axis=1, keepdims=True)
        dscores = (probs * (dprobs - delta)).astype(jnp.bfloat16)
        dq = (dot(dscores, k, NN) * FACTOR).astype(jnp.bfloat16)
        part[:, :d] += dot(dscores, q, TN)
        part[:, d:] += dot(probs_half, g, TN)
        for t, span in enumerate(spans):
            a_ref[i, :, span] = out[t * b : (t + 1) * b]
            dq_ref[i, :, span] = dq[t * b : (t + 1) * b]
        return carry

    lax.fori_loop(0, GROUP // HEADS_AT_ONCE, heads, 0)
    for e in range(slots):
        at = jnp.maximum(slot_ref[i * slots + e], 0)
        total[at, :, :d] += part[e * b : (e + 1) * b, :d] * FACTOR
        total[at, :, d:] += part[e * b : (e + 1) * b, d:]


def cost(blocks, slots, stored, wide):
    return pl.CostEstimate(
        flops=10 * blocks * slots * GROUP * BLOCK_TOKENS * BLOCK_TOKENS * HEAD_SIZE,
        transcendentals=blocks * slots * GROUP * BLOCK_TOKENS * BLOCK_TOKENS,
        bytes_accessed=blocks * BLOCK_TOKENS * GROUP_WIDTH * 8
        + stored * BLOCK_TOKENS * 2 * HEAD_SIZE * (2 + wide),
    )


def scratch(slots):
    return [
        pltpu.VMEM((slots * BLOCK_TOKENS, HEAD_SIZE), jnp.bfloat16),
        pltpu.VMEM((slots * BLOCK_TOKENS, HEAD_SIZE), jnp.bfloat16),
        pltpu.VMEM((slots * BLOCK_TOKENS, 2 * HEAD_SIZE), jnp.float32),
    ]


def plain_kernel(slot_ref, q_ref, g_ref, kv_ref, a_ref, dq_ref, total, keys_at, values_at, part, *, slots):
    total[...] = jnp.zeros_like(total)

    def block(i, carry):
        attend_block(i, slot_ref, q_ref, g_ref, kv_ref, a_ref, dq_ref, total, keys_at, values_at, part, slots)
        return carry

    lax.fori_loop(0, q_ref.shape[0], block, 0)


def plain_attention(slot, q, g, kv, slots):
    whole = pl.BlockSpec(memory_space=pltpu.VMEM)
    like = jax.ShapeDtypeStruct(q.shape, jnp.bfloat16)
    return pl.pallas_call(
        functools.partial(plain_kernel, slots=slots),
        grid_spec=pltpu.PrefetchScalarGridSpec(
            num_scalar_prefetch=1,
            grid=(),
            in_specs=[whole] * 3,
            out_specs=[whole] * 3,
            scratch_shapes=scratch(slots),
        ),
        out_shape=[like, like, jax.ShapeDtypeStruct(kv.shape, jnp.float32)],
        compiler_params=pltpu.CompilerParams(vmem_limit_bytes=60 << 20),
        cost_estimate=cost(q.shape[0], slots, kv.shape[0], 4),
    )(slot, q, g, kv)


def general(queries, keys, values, output_gradient, kv_blocks, block_position):
    query_home, key_home, value_home, grad_home = (
        lax.all_to_all(a, "head", split_axis=2, concat_axis=1, tiled=True)
        for a in (queries, keys, values, output_gradient)
    )
    sequences, tokens, query_width = query_home.shape
    kv_heads = key_home.shape[2] // HEAD_SIZE
    per_device = tokens // BLOCK_TOKENS
    slots = kv_blocks.shape[1]
    my_index = lax.axis_index("seq")
    located = stored_index(block_position)
    my_blocks = lax.dynamic_slice_in_dim(block_position, my_index * per_device, per_device)
    listed = jnp.take(kv_blocks, my_blocks, axis=0).reshape(-1)
    slot = jnp.where(listed >= 0, jnp.take(located, jnp.maximum(listed, 0)), -1)
    outs = []
    for sequence in range(sequences):
        heads = []
        for head in range(kv_heads):
            wide = slice(head * GROUP_WIDTH, (head + 1) * GROUP_WIDTH)
            narrow = slice(head * HEAD_SIZE, (head + 1) * HEAD_SIZE)
            kv = jnp.concatenate([key_home[sequence, :, narrow], value_home[sequence, :, narrow]], axis=1)
            kv = lax.all_gather(kv, "seq", axis=0, tiled=True)
            kv = kv.reshape(-1, BLOCK_TOKENS, 2 * HEAD_SIZE)
            q = query_home[sequence, :, wide].reshape(per_device, BLOCK_TOKENS, GROUP_WIDTH)
            g = grad_home[sequence, :, wide].reshape(per_device, BLOCK_TOKENS, GROUP_WIDTH)
            attention, query_grad, total = plain_attention(slot, q, g, kv, slots)
            total = lax.psum_scatter(total, "seq", scatter_dimension=0, tiled=True)
            total = total.astype(jnp.bfloat16).reshape(tokens, 2 * HEAD_SIZE)
            heads.append(
                (
                    attention.reshape(tokens, GROUP_WIDTH),
                    query_grad.reshape(tokens, GROUP_WIDTH),
                    total[:, :HEAD_SIZE],
                    total[:, HEAD_SIZE:],
                )
            )
        outs.append(tuple(jnp.concatenate(parts, axis=1) for parts in zip(*heads)))
    return tuple(jnp.stack(parts) for parts in zip(*outs))


def quad_kernel(slot_ref, meta_ref, *refs, slots, lines, columns):
    q_pieces, refs = refs[:4], refs[4:]
    g_pieces, refs = refs[:4], refs[4:]
    arrivals = 2 + 4 * (lines - 1)
    kv_pieces, refs = refs[:arrivals], refs[arrivals:]
    a_out, dq_out, total_out = refs[:3]
    q_at, g_at, kv_at, a_at, dq_at, total, keys_at, values_at, part, kv_sem, in_sem, out_sem = refs[3:]
    z, x, h, column = meta_ref[0], meta_ref[1], meta_ref[2], meta_ref[3]
    copies = []
    for n, ref in enumerate(kv_pieces):
        if n < 2:
            step, side, good = 0, n, None
        else:
            step, kind = 1 + (n - 2) // 4, (n - 2) % 4
            side = kind // 2
            good = (z >= step) if kind % 2 == 0 else (z + step < lines)
            step = -step if kind % 2 == 0 else step
        there = (z + step) * 2 + (x if side == 0 else 1 - x)
        copies.append((good, pltpu.make_async_copy(ref, kv_at.at[pl.ds(there * 4, 4)], kv_sem.at[n])))

    def each(act):
        for good, copy in copies:
            if good is None:
                act(copy)
            else:
                pl.when(good)(functools.partial(act, copy))

    each(lambda copy: copy.start())
    span = pl.ds(pl.multiple_of(column * GROUP_WIDTH, GROUP_WIDTH), GROUP_WIDTH)
    inward = []
    for n in range(4):
        for ref, at, which in ((q_pieces[n], q_at, 0), (g_pieces[n], g_at, 1)):
            source = ref.at[0, :, span] if n == 0 else ref
            inward.append(pltpu.make_async_copy(source, at.at[n], in_sem.at[which, n]))
            inward[-1].start()
    total[...] = jnp.zeros_like(total)
    each(lambda copy: copy.wait())
    for copy in inward:
        copy.wait()

    def block(i, carry):
        attend_block(i, slot_ref, q_at, g_at, kv_at, a_at, dq_at, total, keys_at, values_at, part, slots)
        place = i // 2
        row = pl.ds(pl.multiple_of((h ^ (i & 1)) * BLOCK_TOKENS, BLOCK_TOKENS), BLOCK_TOKENS)
        pltpu.make_async_copy(a_at.at[i], a_out.at[place, row], out_sem.at[0]).start()
        pltpu.make_async_copy(dq_at.at[i], dq_out.at[place, row], out_sem.at[1]).start()
        return carry

    lax.fori_loop(0, 4, block, 0)
    total_out[...] = total[...].astype(jnp.bfloat16)
    pltpu.make_async_copy(a_out, a_out, out_sem.at[0]).wait()
    pltpu.make_async_copy(dq_out, dq_out, out_sem.at[1]).wait()


def quad_attention(slot, meta, q_pieces, g_pieces, kv_pieces, slots, lines):
    anywhere = pl.BlockSpec(memory_space=pl.ANY)
    stored = lines * 2 * 4
    out = jax.ShapeDtypeStruct((2, 2 * BLOCK_TOKENS, GROUP_WIDTH), jnp.bfloat16)
    wide = pltpu.VMEM((4, BLOCK_TOKENS, GROUP_WIDTH), jnp.bfloat16)
    return pl.pallas_call(
        functools.partial(quad_kernel, slots=slots, lines=lines, columns=GROUP_WIDTH),
        grid_spec=pltpu.PrefetchScalarGridSpec(
            num_scalar_prefetch=2,
            grid=(),
            in_specs=[anywhere] * (8 + len(kv_pieces)),
            out_specs=[anywhere, anywhere, pl.BlockSpec(memory_space=pltpu.VMEM)],
            scratch_shapes=[
                wide,
                wide,
                pltpu.VMEM((stored, BLOCK_TOKENS, 2 * HEAD_SIZE), jnp.bfloat16),
                wide,
                wide,
                pltpu.VMEM((stored, BLOCK_TOKENS, 2 * HEAD_SIZE), jnp.float32),
                *scratch(slots),
                pltpu.SemaphoreType.DMA((len(kv_pieces),)),
                pltpu.SemaphoreType.DMA((2, 4)),
                pltpu.SemaphoreType.DMA((2,)),
            ],
        ),
        out_shape=[out, out, jax.ShapeDtypeStruct((stored, BLOCK_TOKENS, 2 * HEAD_SIZE), jnp.bfloat16)],
        compiler_params=pltpu.CompilerParams(vmem_limit_bytes=40 << 20),
        cost_estimate=cost(4, slots, stored, 2),
    )(slot, meta, *q_pieces, *g_pieces, *kv_pieces)


def quad(queries, keys, values, output_gradient, kv_blocks, block_position):
    seq_count = lax.axis_size("seq")
    lines = seq_count // 4
    slots = kv_blocks.shape[1]
    s = lax.axis_index("seq")
    h = lax.axis_index("head")
    c = s % 2
    chip = s // 2
    z, x = chip // 2, chip % 2
    kv_heads = keys.shape[2] // HEAD_SIZE // 4
    located = stored_index(block_position)
    across = [(0, 1), (1, 0)]
    beside = [(i, i ^ 1) for i in range(seq_count)]
    corner = [(i * 2 + j, (i ^ 1) * 2 + 1 - j) for i in range(seq_count) for j in range(2)]

    def trade(slices):
        return [
            slices(h, c),
            lax.ppermute(slices(1 - h, c), "head", across),
            lax.ppermute(slices(h, 1 - c), "seq", beside),
            lax.ppermute(slices(1 - h, 1 - c), ("seq", "head"), corner),
        ]

    def kv_slices(hh, cc):
        width = kv_heads * HEAD_SIZE
        start = (hh * 2 + cc) * width
        k = lax.dynamic_slice_in_dim(keys[0], start, width, axis=1)
        v = lax.dynamic_slice_in_dim(values[0], start, width, axis=1)
        k = k.reshape(BLOCK_TOKENS, kv_heads, HEAD_SIZE)
        v = v.reshape(BLOCK_TOKENS, kv_heads, HEAD_SIZE)
        return jnp.moveaxis(jnp.concatenate([k, v], axis=2), 1, 0)

    kv_traded = trade(kv_slices)
    order = [(0, 0), (0, 1), (1, 0), (1, 1)]
    blocks = jnp.stack([chip * 4 + 2 * (c ^ dc) + (h ^ dy) for dc, dy in order])
    listed = jnp.take(kv_blocks, jnp.take(block_position, blocks), axis=0).reshape(-1)
    home = jnp.take(located, jnp.maximum(listed, 0))
    piece = (((home % 4) // 2) ^ c) * 2 + ((home % 2) ^ h)
    slot = jnp.where(listed >= 0, (home // 4) * 4 + piece, -1).astype(jnp.int32)

    def sideways(first, last):
        return [
            (zz * 4 + xx * 2 + cc, zz * 4 + (1 - xx) * 2 + cc)
            for zz in range(first, last)
            for xx in range(2)
            for cc in range(2)
        ]

    def gather(own):
        arrived = [own, lax.ppermute(own, "seq", sideways(0, lines))]
        up = down = own
        for t in range(1, lines):
            up = lax.ppermute(up, "seq", [(zz * 4 + r, zz * 4 + 4 + r) for zz in range(t - 1, lines - 1) for r in range(4)])
            down = lax.ppermute(down, "seq", [(zz * 4 + 4 + r, zz * 4 + r) for zz in range(lines - t) for r in range(4)])
            arrived += [
                up,
                down,
                lax.ppermute(up, "seq", sideways(t, lines)),
                lax.ppermute(down, "seq", sideways(0, lines - t)),
            ]
        return arrived

    same = [[zz * 4 + xx * 2 + cc for zz in range(lines) for xx in range(2)] for cc in range(2)]
    own_parts = []
    far_parts = []
    grad_parts = []
    for head in range(kv_heads):
        kv_own = jnp.stack([part[head] for part in kv_traded])
        kv_pieces = gather(kv_own)

        def wide_slices(array):
            def slices(hh, cc):
                start = ((hh * 2 + cc) * kv_heads + head) * GROUP_WIDTH
                return lax.dynamic_slice_in_dim(array[0], start, GROUP_WIDTH, axis=1)

            return slices

        q_pieces = [queries] + trade(wide_slices(queries))[1:]
        g_pieces = [output_gradient] + trade(wide_slices(output_gradient))[1:]
        meta = jnp.stack([z, x, h, (h * 2 + c) * kv_heads + head]).astype(jnp.int32)
        attention, query_grad, total = quad_attention(slot, meta, q_pieces, g_pieces, kv_pieces, slots, lines)
        far = jnp.stack([attention[1], query_grad[1]])
        far_parts.append(lax.ppermute(far, "seq", beside))
        own_parts.append((attention[0], query_grad[0]))
        returned = lax.all_to_all(
            total.reshape(lines * 2, -1, 2 * HEAD_SIZE), "seq", split_axis=0, concat_axis=0, tiled=True, axis_index_groups=same
        )
        summed = jnp.sum(returned.astype(jnp.float32), axis=0).astype(jnp.bfloat16)
        summed = summed.reshape(2, 2, BLOCK_TOKENS, 2 * HEAD_SIZE)
        grad_parts.append((summed[0], lax.ppermute(summed[1], "seq", beside)))

    def place(own, far):
        return jnp.where(c == 0, jnp.concatenate(own + far, axis=-1), jnp.concatenate(far + own, axis=-1))[None]

    outs = [
        place([part[n] for part in own_parts], [part[n] for part in far_parts])
        for n in range(2)
    ]
    for n in range(2):
        span = slice(n * HEAD_SIZE, (n + 1) * HEAD_SIZE)
        grad = place([part[0][..., span] for part in grad_parts], [part[1][..., span] for part in grad_parts])[0]
        grad = jnp.where(h == 0, grad, grad[::-1])
        outs.append(grad.reshape(1, 2 * BLOCK_TOKENS, -1))
    return tuple(outs)


def body(queries, keys, values, output_gradient, kv_blocks, block_position):
    sequences, tokens, _ = queries.shape
    fits = (
        lax.axis_size("head") == 2
        and lax.axis_size("seq") % 4 == 0
        and sequences == 1
        and tokens == BLOCK_TOKENS
        and KEY_VALUE_HEADS % 4 == 0
    )
    chosen = quad if fits else general
    return chosen(queries, keys, values, output_gradient, kv_blocks, block_position)


def solution(mesh):
    placed = (
        P(None, ("seq", "head"), None),
        P(None, ("seq", "head"), None),
        P(None, ("seq", "head"), None),
        P(None, ("seq", "head"), None),
        P(),
        P(),
    )
    return jax.shard_map(
        body,
        mesh=mesh,
        in_specs=placed,
        out_specs=(
            P(None, "seq", "head"),
            P(None, "seq", "head"),
            P(None, "seq", "head"),
            P(None, "seq", "head"),
        ),
        check_vma=False,
    )
```

```python
import functools

import jax
import jax.numpy as jnp
from jax import lax
from jax.experimental import pallas as pl
from jax.experimental.pallas import tpu as pltpu
from jax.sharding import PartitionSpec as P

QUERY_HEADS = 64
KEY_VALUE_HEADS = 8
HEAD_SIZE = 128
BLOCK_TOKENS = 128
GLOB = 2
GROUP = QUERY_HEADS // KEY_VALUE_HEADS
GROUP_WIDTH = GROUP * HEAD_SIZE
HEADS_AT_ONCE = 4
LOG2E = 1.4426950408889634
FACTOR = HEAD_SIZE ** (-0.5)


NT = (((1,), (1,)), ((), ()))
TN = (((0,), (0,)), ((), ()))
NN = (((1,), (0,)), ((), ()))


def dot(a, b, dims):
    return lax.dot_general(a, b, dims, preferred_element_type=jnp.float32)


def stored_index(block_position):
    block_list = block_position.shape[0]
    stored = jnp.arange(block_list, dtype=jnp.int32)
    matches = block_position[None, :] == stored[:, None]
    return jnp.sum(jnp.where(matches, stored[None, :], 0), axis=1)


def attend_block(i, slot_ref, q_ref, g_ref, kv_ref, a_ref, dq_ref, total, keys_at, values_at, part, slots):
    b = BLOCK_TOKENS
    d = HEAD_SIZE
    rows = HEADS_AT_ONCE * b
    for e in range(slots):
        at = jnp.maximum(slot_ref[i * slots + e], 0)
        keys_at[e * b : (e + 1) * b, :] = kv_ref[at, :, :d]
        values_at[e * b : (e + 1) * b, :] = kv_ref[at, :, d:]
    bias = [
        jnp.where(slot_ref[i * slots + e] >= 0, 0.0, jnp.inf).astype(jnp.float32) for e in range(slots)
    ]
    part[...] = jnp.zeros_like(part)

    def heads(j, carry):
        spans = [pl.ds((j * HEADS_AT_ONCE + t) * d, d) for t in range(HEADS_AT_ONCE)]
        q = jnp.concatenate([q_ref[i, :, span] for span in spans], axis=0)
        g = jnp.concatenate([g_ref[i, :, span] for span in spans], axis=0)
        k = keys_at[...]
        v = values_at[...]
        s = dot(q, k, NT)
        column = lax.broadcasted_iota(jnp.int32, (rows, b), 1)
        row = lax.broadcasted_iota(jnp.int32, (rows, b), 0) & (b - 1)
        tiles = [jnp.where(column <= row, s[:, :b], -jnp.inf)]
        tiles += [s[:, e * b : (e + 1) * b] for e in range(1, slots)]
        high = tiles[0]
        for e in range(1, slots):
            high = jnp.maximum(high, tiles[e] - bias[e])
        high = jnp.max(high, axis=1, keepdims=True) * (FACTOR * LOG2E)
        powers = [jnp.exp2(tiles[e] * (FACTOR * LOG2E) - (high + bias[e])) for e in range(slots)]
        inverse = 1.0 / jnp.sum(functools.reduce(jnp.add, powers), axis=1, keepdims=True)
        probs = jnp.concatenate([power * inverse for power in powers], axis=1)
        probs_half = probs.astype(jnp.bfloat16)
        out = dot(probs_half, v, NN).astype(jnp.bfloat16)
        dprobs = dot(g, v, NT)
        delta = jnp.sum(g.astype(jnp.float32) * out.astype(jnp.float32), axis=1, keepdims=True)
        dscores = (probs * (dprobs - delta)).astype(jnp.bfloat16)
        dq = (dot(dscores, k, NN) * FACTOR).astype(jnp.bfloat16)
        part[:, :d] += dot(dscores, q, TN)
        part[:, d:] += dot(probs_half, g, TN)
        for t, span in enumerate(spans):
            a_ref[i, :, span] = out[t * b : (t + 1) * b]
            dq_ref[i, :, span] = dq[t * b : (t + 1) * b]
        return carry

    lax.fori_loop(0, GROUP // HEADS_AT_ONCE, heads, 0)
    for e in range(slots):
        at = jnp.maximum(slot_ref[i * slots + e], 0)
        total[at, :, :d] += part[e * b : (e + 1) * b, :d] * FACTOR
        total[at, :, d:] += part[e * b : (e + 1) * b, d:]


def cost(blocks, slots, stored, wide):
    return pl.CostEstimate(
        flops=10 * blocks * slots * GROUP * BLOCK_TOKENS * BLOCK_TOKENS * HEAD_SIZE,
        transcendentals=blocks * slots * GROUP * BLOCK_TOKENS * BLOCK_TOKENS,
        bytes_accessed=blocks * BLOCK_TOKENS * GROUP_WIDTH * 8
        + stored * BLOCK_TOKENS * 2 * HEAD_SIZE * (2 + wide),
    )


def scratch(slots):
    return [
        pltpu.VMEM((slots * BLOCK_TOKENS, HEAD_SIZE), jnp.bfloat16),
        pltpu.VMEM((slots * BLOCK_TOKENS, HEAD_SIZE), jnp.bfloat16),
        pltpu.VMEM((slots * BLOCK_TOKENS, 2 * HEAD_SIZE), jnp.float32),
    ]


def plain_kernel(slot_ref, q_ref, g_ref, kv_ref, a_ref, dq_ref, total, keys_at, values_at, part, *, slots):
    total[...] = jnp.zeros_like(total)

    def block(i, carry):
        attend_block(i, slot_ref, q_ref, g_ref, kv_ref, a_ref, dq_ref, total, keys_at, values_at, part, slots)
        return carry

    lax.fori_loop(0, q_ref.shape[0], block, 0)


def plain_attention(slot, q, g, kv, slots):
    whole = pl.BlockSpec(memory_space=pltpu.VMEM)
    like = jax.ShapeDtypeStruct(q.shape, jnp.bfloat16)
    return pl.pallas_call(
        functools.partial(plain_kernel, slots=slots),
        grid_spec=pltpu.PrefetchScalarGridSpec(
            num_scalar_prefetch=1,
            grid=(),
            in_specs=[whole] * 3,
            out_specs=[whole] * 3,
            scratch_shapes=scratch(slots),
        ),
        out_shape=[like, like, jax.ShapeDtypeStruct(kv.shape, jnp.float32)],
        compiler_params=pltpu.CompilerParams(vmem_limit_bytes=60 << 20),
        cost_estimate=cost(q.shape[0], slots, kv.shape[0], 4),
    )(slot, q, g, kv)


def general(queries, keys, values, output_gradient, kv_blocks, block_position):
    query_home, key_home, value_home, grad_home = (
        lax.all_to_all(a, "head", split_axis=2, concat_axis=1, tiled=True)
        for a in (queries, keys, values, output_gradient)
    )
    sequences, tokens, query_width = query_home.shape
    kv_heads = key_home.shape[2] // HEAD_SIZE
    per_device = tokens // BLOCK_TOKENS
    slots = kv_blocks.shape[1]
    my_index = lax.axis_index("seq")
    located = stored_index(block_position)
    my_blocks = lax.dynamic_slice_in_dim(block_position, my_index * per_device, per_device)
    listed = jnp.take(kv_blocks, my_blocks, axis=0).reshape(-1)
    slot = jnp.where(listed >= 0, jnp.take(located, jnp.maximum(listed, 0)), -1)
    outs = []
    for sequence in range(sequences):
        heads = []
        for head in range(kv_heads):
            wide = slice(head * GROUP_WIDTH, (head + 1) * GROUP_WIDTH)
            narrow = slice(head * HEAD_SIZE, (head + 1) * HEAD_SIZE)
            kv = jnp.concatenate([key_home[sequence, :, narrow], value_home[sequence, :, narrow]], axis=1)
            kv = lax.all_gather(kv, "seq", axis=0, tiled=True)
            kv = kv.reshape(-1, BLOCK_TOKENS, 2 * HEAD_SIZE)
            q = query_home[sequence, :, wide].reshape(per_device, BLOCK_TOKENS, GROUP_WIDTH)
            g = grad_home[sequence, :, wide].reshape(per_device, BLOCK_TOKENS, GROUP_WIDTH)
            attention, query_grad, total = plain_attention(slot, q, g, kv, slots)
            total = lax.psum_scatter(total, "seq", scatter_dimension=0, tiled=True)
            total = total.astype(jnp.bfloat16).reshape(tokens, 2 * HEAD_SIZE)
            heads.append(
                (
                    attention.reshape(tokens, GROUP_WIDTH),
                    query_grad.reshape(tokens, GROUP_WIDTH),
                    total[:, :HEAD_SIZE],
                    total[:, HEAD_SIZE:],
                )
            )
        outs.append(tuple(jnp.concatenate(parts, axis=1) for parts in zip(*heads)))
    return tuple(jnp.stack(parts) for parts in zip(*outs))


def quad_kernel(listed_ref, position_ref, q_ref, g_ref, *refs, slots, lines, kv_heads, head):
    pieces, refs = refs[:3], refs[3:]
    kv_line, kv_beside, a_own, dq_own, far, total_line, total_beside = refs[:7]
    located, slot, q_at, g_at, kv_at, a_at, dq_at, total, keys_at, values_at, part, kv_sem, in_sem, out_sem = refs[7:]
    s = lax.axis_index("seq")
    h = lax.axis_index("head")
    x = (s >> 1) & 1
    half = lines * 4
    fetches = [
        pltpu.make_async_copy(ref, kv_at.at[pl.ds(n * half, half)], kv_sem.at[n])
        for n, ref in enumerate((kv_line, kv_beside))
    ]
    column = (h * 2 + x) * kv_heads + head
    span = pl.ds(pl.multiple_of(column * GROUP_WIDTH, GROUP_WIDTH), GROUP_WIDTH)
    for which, (ref, at) in enumerate(((q_ref, q_at), (g_ref, g_at))):
        fetches.append(pltpu.make_async_copy(ref.at[0, :, span], at.at[0], in_sem.at[which, 0]))
        for n in range(3):
            fetches.append(pltpu.make_async_copy(pieces[n].at[which], at.at[n + 1], in_sem.at[which, n + 1]))
    for fetch in fetches:
        fetch.start()

    def locate(j, carry):
        located[position_ref[j]] = j
        return carry

    lax.fori_loop(0, lines * 8, locate, 0)

    def entry(n, carry):
        i, e = n // slots, n % slots
        stored = ((s ^ (2 * (i >> 1))) * 2) + (h ^ (i & 1))
        b = listed_ref[position_ref[stored], e]
        home = located[jnp.maximum(b, 0)]
        seq_home = home >> 1
        where_ = ((seq_home ^ s) & 1) * half + (seq_home >> 2) * 4
        where_ = where_ + (((seq_home >> 1) & 1) ^ x) * 2 + ((home & 1) ^ h)
        slot[n] = jnp.where(b >= 0, where_, -1)
        return carry

    lax.fori_loop(0, 4 * slots, entry, 0)
    total[...] = jnp.zeros_like(total)
    for fetch in fetches:
        fetch.wait()

    def block(i, carry):
        attend_block(i, slot, q_at, g_at, kv_at, a_at, dq_at, total, keys_at, values_at, part, slots)
        row = pl.ds(pl.multiple_of((h ^ (i & 1)) * BLOCK_TOKENS, BLOCK_TOKENS), BLOCK_TOKENS)

        @pl.when(i < 2)
        def _():
            pltpu.make_async_copy(a_at.at[i], a_own.at[row], out_sem.at[0]).start()
            pltpu.make_async_copy(dq_at.at[i], dq_own.at[row], out_sem.at[1]).start()

        @pl.when(i >= 2)
        def _():
            pltpu.make_async_copy(a_at.at[i], far.at[0, row], out_sem.at[2]).start()
            pltpu.make_async_copy(dq_at.at[i], far.at[1, row], out_sem.at[2]).start()

        return carry

    lax.fori_loop(0, 4, block, 0)
    total_line[...] = total[:half].astype(jnp.bfloat16)
    total_beside[...] = total[half:].astype(jnp.bfloat16)
    for n, ref in enumerate((a_own, dq_own, far)):
        pltpu.make_async_copy(ref, ref, out_sem.at[n]).wait()


def quad_attention(kv_blocks, block_position, queries, output_gradient, pieces, kv_line, kv_beside, lines, kv_heads, head):
    outside = pl.BlockSpec(memory_space=pltpu.HBM)
    inside = pl.BlockSpec(memory_space=pltpu.VMEM)
    slots = kv_blocks.shape[1]
    half = lines * 4
    own = jax.ShapeDtypeStruct((2 * BLOCK_TOKENS, GROUP_WIDTH), jnp.bfloat16)
    sums = jax.ShapeDtypeStruct((half, BLOCK_TOKENS, 2 * HEAD_SIZE), jnp.bfloat16)
    wide = pltpu.VMEM((4, BLOCK_TOKENS, GROUP_WIDTH), jnp.bfloat16)
    return pl.pallas_call(
        functools.partial(quad_kernel, slots=slots, lines=lines, kv_heads=kv_heads, head=head),
        grid_spec=pltpu.PrefetchScalarGridSpec(
            num_scalar_prefetch=2,
            grid=(),
            in_specs=[outside] * 7,
            out_specs=[outside] * 3 + [inside] * 2,
            scratch_shapes=[
                pltpu.SMEM((lines * 8,), jnp.int32),
                pltpu.SMEM((4 * slots,), jnp.int32),
                wide,
                wide,
                pltpu.VMEM((2 * half, BLOCK_TOKENS, 2 * HEAD_SIZE), jnp.bfloat16),
                wide,
                wide,
                pltpu.VMEM((2 * half, BLOCK_TOKENS, 2 * HEAD_SIZE), jnp.float32),
                *scratch(slots),
                pltpu.SemaphoreType.DMA((2,)),
                pltpu.SemaphoreType.DMA((2, 4)),
                pltpu.SemaphoreType.DMA((3,)),
            ],
        ),
        out_shape=[own, own, jax.ShapeDtypeStruct((2, *own.shape), jnp.bfloat16), sums, sums],
        compiler_params=pltpu.CompilerParams(vmem_limit_bytes=48 << 20),
        cost_estimate=cost(4, slots, 2 * half, 2),
    )(kv_blocks, block_position, queries, output_gradient, *pieces, kv_line, kv_beside)


def quad(queries, keys, values, output_gradient, kv_blocks, block_position):
    seq_count = lax.axis_size("seq")
    lines = seq_count // 4
    s = lax.axis_index("seq")
    h = lax.axis_index("head")
    x = (s // 2) % 2
    kv_heads = keys.shape[2] // HEAD_SIZE // 4
    across = [(0, 1), (1, 0)]
    beside = [(i, i ^ 1) for i in range(seq_count)]
    sideways = [(i, i ^ 2) for i in range(seq_count)]
    corner = [(i * 2 + j, (i ^ 2) * 2 + 1 - j) for i in range(seq_count) for j in range(2)]
    line_groups = [[line * 4 + r for line in range(lines)] for r in range(4)]

    def trade(slices):
        return [
            lax.ppermute(slices(1 - h, x), "head", across),
            lax.ppermute(slices(h, 1 - x), "seq", sideways),
            lax.ppermute(slices(1 - h, 1 - x), ("seq", "head"), corner),
        ]

    def along_line(array):
        return lax.all_to_all(array, "seq", split_axis=0, concat_axis=0, tiled=True, axis_index_groups=line_groups)

    def kv_slices(hh, xx):
        width = kv_heads * HEAD_SIZE
        start = (hh * 2 + xx) * width
        k = lax.dynamic_slice_in_dim(keys[0], start, width, axis=1)
        v = lax.dynamic_slice_in_dim(values[0], start, width, axis=1)
        k = k.reshape(BLOCK_TOKENS, kv_heads, HEAD_SIZE)
        v = v.reshape(BLOCK_TOKENS, kv_heads, HEAD_SIZE)
        return jnp.moveaxis(jnp.concatenate([k, v], axis=2), 1, 0)

    def wide_slices(head):
        def slices(hh, xx):
            start = ((hh * 2 + xx) * kv_heads + head) * GROUP_WIDTH
            return jnp.stack(
                [lax.dynamic_slice_in_dim(a[0], start, GROUP_WIDTH, axis=1) for a in (queries, output_gradient)]
            )

        return slices

    kv_traded = [kv_slices(h, x)] + trade(kv_slices)
    pieces = [trade(wide_slices(head)) for head in range(kv_heads)]
    kv_lines = []
    for head in range(kv_heads):
        own = jnp.stack([part[head] for part in kv_traded])
        with jax.named_scope("gather%d" % head):
            kv_lines.append(along_line(jnp.concatenate([own] * lines)))
    own_parts = []
    far_parts = []
    grad_parts = []
    for head in range(kv_heads):
        kv_beside = lax.ppermute(kv_lines[head], "seq", beside)
        with jax.named_scope("attend%d" % head):
            a_own, dq_own, far, total_line, total_beside = quad_attention(
                kv_blocks, block_position, queries, output_gradient, pieces[head], kv_lines[head], kv_beside, lines, kv_heads, head
            )
        arrived = lax.ppermute(total_beside, "seq", beside)
        far_parts.append(lax.ppermute(far, "seq", sideways))
        own_parts.append((a_own, dq_own))
        total = total_line.astype(jnp.float32) + arrived.astype(jnp.float32)
        with jax.named_scope("home%d" % head):
            returned = along_line(total.astype(jnp.bfloat16))
        returned = returned.reshape(lines, 2, 2, BLOCK_TOKENS, 2 * HEAD_SIZE)
        summed = jnp.sum(returned.astype(jnp.float32), axis=0).astype(jnp.bfloat16)
        grad_parts.append((summed[0], lax.ppermute(summed[1], "seq", sideways)))

    def place(own, far):
        return jnp.where(x == 0, jnp.concatenate(own + far, axis=-1), jnp.concatenate(far + own, axis=-1))

    outs = [place([part[n] for part in own_parts], [part[n] for part in far_parts])[None] for n in range(2)]
    for n in range(2):
        span = slice(n * HEAD_SIZE, (n + 1) * HEAD_SIZE)
        grad = place([part[0][..., span] for part in grad_parts], [part[1][..., span] for part in grad_parts])
        grad = jnp.where(h == 0, grad, grad[::-1])
        outs.append(grad.reshape(1, 2 * BLOCK_TOKENS, -1))
    return tuple(outs)


def body(queries, keys, values, output_gradient, kv_blocks, block_position):
    sequences, tokens, _ = queries.shape
    fits = (
        lax.axis_size("head") == 2
        and lax.axis_size("seq") % 4 == 0
        and sequences == 1
        and tokens == BLOCK_TOKENS
        and KEY_VALUE_HEADS % 4 == 0
    )
    chosen = quad if fits else general
    return chosen(queries, keys, values, output_gradient, kv_blocks, block_position)


def solution(mesh):
    placed = (
        P(None, ("seq", "head"), None),
        P(None, ("seq", "head"), None),
        P(None, ("seq", "head"), None),
        P(None, ("seq", "head"), None),
        P(),
        P(),
    )
    return jax.shard_map(
        body,
        mesh=mesh,
        in_specs=placed,
        out_specs=(
            P(None, "seq", "head"),
            P(None, "seq", "head"),
            P(None, "seq", "head"),
            P(None, "seq", "head"),
        ),
        check_vma=False,
    )
```

```python
import functools

import jax
import jax.numpy as jnp
from jax import lax
from jax.experimental import pallas as pl
from jax.experimental.pallas import tpu as pltpu
from jax.sharding import PartitionSpec as P


QUERY_HEADS = 64
KEY_VALUE_HEADS = 8
HEAD_SIZE = 128
BLOCK_TOKENS = 128
GROUP = QUERY_HEADS // KEY_VALUE_HEADS
GROUP_WIDTH = GROUP * HEAD_SIZE
HEADS_AT_ONCE = 4
LOG2E = 1.4426950408889634
FACTOR = HEAD_SIZE ** (-0.5)


NT = (((1,), (1,)), ((), ()))
TN = (((0,), (0,)), ((), ()))
NN = (((1,), (0,)), ((), ()))


def dot(a, b, dims):
    return lax.dot_general(a, b, dims, preferred_element_type=jnp.float32)


def stored_index(block_position):
    block_list = block_position.shape[0]
    stored = jnp.arange(block_list, dtype=jnp.int32)
    matches = block_position[None, :] == stored[:, None]
    return jnp.sum(jnp.where(matches, stored[None, :], 0), axis=1)


def attend_block(i, slot_ref, q_ref, g_ref, kv_ref, a_ref, dq_ref, total, keys_at, values_at, part, slots):
    b = BLOCK_TOKENS
    d = HEAD_SIZE
    rows = HEADS_AT_ONCE * b
    for e in range(slots):
        at = jnp.maximum(slot_ref[i * slots + e], 0)
        keys_at[e * b : (e + 1) * b, :] = kv_ref[at, :, :d]
        values_at[e * b : (e + 1) * b, :] = kv_ref[at, :, d:]
    bias = [
        jnp.where(slot_ref[i * slots + e] >= 0, 0.0, jnp.inf).astype(jnp.float32) for e in range(slots)
    ]
    part[...] = jnp.zeros_like(part)

    def heads(j, carry):
        spans = [pl.ds((j * HEADS_AT_ONCE + t) * d, d) for t in range(HEADS_AT_ONCE)]
        q = jnp.concatenate([q_ref[i, :, span] for span in spans], axis=0)
        g = jnp.concatenate([g_ref[i, :, span] for span in spans], axis=0)
        k = keys_at[...]
        v = values_at[...]
        s = dot(q, k, NT)
        column = lax.broadcasted_iota(jnp.int32, (rows, b), 1)
        row = lax.broadcasted_iota(jnp.int32, (rows, b), 0) & (b - 1)
        tiles = [jnp.where(column <= row, s[:, :b], -jnp.inf)]
        tiles += [s[:, e * b : (e + 1) * b] for e in range(1, slots)]
        high = tiles[0]
        for e in range(1, slots):
            high = jnp.maximum(high, tiles[e] - bias[e])
        high = jnp.max(high, axis=1, keepdims=True) * (FACTOR * LOG2E)
        powers = [jnp.exp2(tiles[e] * (FACTOR * LOG2E) - (high + bias[e])) for e in range(slots)]
        inverse = 1.0 / jnp.sum(functools.reduce(jnp.add, powers), axis=1, keepdims=True)
        probs = jnp.concatenate([power * inverse for power in powers], axis=1)
        probs_half = probs.astype(jnp.bfloat16)
        out = dot(probs_half, v, NN).astype(jnp.bfloat16)
        dprobs = dot(g, v, NT)
        delta = jnp.sum(g.astype(jnp.float32) * out.astype(jnp.float32), axis=1, keepdims=True)
        dscores = (probs * (dprobs - delta)).astype(jnp.bfloat16)
        dq = (dot(dscores, k, NN) * FACTOR).astype(jnp.bfloat16)
        part[:, :d] += dot(dscores, q, TN)
        part[:, d:] += dot(probs_half, g, TN)
        for t, span in enumerate(spans):
            a_ref[i, :, span] = out[t * b : (t + 1) * b]
            dq_ref[i, :, span] = dq[t * b : (t + 1) * b]
        return carry

    lax.fori_loop(0, GROUP // HEADS_AT_ONCE, heads, 0)
    for e in range(slots):
        at = jnp.maximum(slot_ref[i * slots + e], 0)
        total[at, :, :d] += part[e * b : (e + 1) * b, :d] * FACTOR
        total[at, :, d:] += part[e * b : (e + 1) * b, d:]


def cost(blocks, slots, stored, wide):
    return pl.CostEstimate(
        flops=10 * blocks * slots * GROUP * BLOCK_TOKENS * BLOCK_TOKENS * HEAD_SIZE,
        transcendentals=blocks * slots * GROUP * BLOCK_TOKENS * BLOCK_TOKENS,
        bytes_accessed=blocks * BLOCK_TOKENS * GROUP_WIDTH * 8
        + stored * BLOCK_TOKENS * 2 * HEAD_SIZE * (2 + wide),
    )


def scratch(slots):
    return [
        pltpu.VMEM((slots * BLOCK_TOKENS, HEAD_SIZE), jnp.bfloat16),
        pltpu.VMEM((slots * BLOCK_TOKENS, HEAD_SIZE), jnp.bfloat16),
        pltpu.VMEM((slots * BLOCK_TOKENS, 2 * HEAD_SIZE), jnp.float32),
    ]


def plain_kernel(slot_ref, q_ref, g_ref, kv_ref, a_ref, dq_ref, total, keys_at, values_at, part, *, slots):
    total[...] = jnp.zeros_like(total)

    def block(i, carry):
        attend_block(i, slot_ref, q_ref, g_ref, kv_ref, a_ref, dq_ref, total, keys_at, values_at, part, slots)
        return carry

    lax.fori_loop(0, q_ref.shape[0], block, 0)


def plain_attention(slot, q, g, kv, slots):
    whole = pl.BlockSpec(memory_space=pltpu.VMEM)
    like = jax.ShapeDtypeStruct(q.shape, jnp.bfloat16)
    return pl.pallas_call(
        functools.partial(plain_kernel, slots=slots),
        grid_spec=pltpu.PrefetchScalarGridSpec(
            num_scalar_prefetch=1,
            grid=(),
            in_specs=[whole] * 3,
            out_specs=[whole] * 3,
            scratch_shapes=scratch(slots),
        ),
        out_shape=[like, like, jax.ShapeDtypeStruct(kv.shape, jnp.float32)],
        compiler_params=pltpu.CompilerParams(vmem_limit_bytes=60 << 20),
        cost_estimate=cost(q.shape[0], slots, kv.shape[0], 4),
    )(slot, q, g, kv)


def general(queries, keys, values, output_gradient, kv_blocks, block_position):
    query_home, key_home, value_home, grad_home = (
        lax.all_to_all(a, "head", split_axis=2, concat_axis=1, tiled=True)
        for a in (queries, keys, values, output_gradient)
    )
    sequences, tokens, _ = query_home.shape
    kv_heads = key_home.shape[2] // HEAD_SIZE
    per_device = tokens // BLOCK_TOKENS
    slots = kv_blocks.shape[1]
    my_index = lax.axis_index("seq")
    located = stored_index(block_position)
    my_blocks = lax.dynamic_slice_in_dim(block_position, my_index * per_device, per_device)
    listed = jnp.take(kv_blocks, my_blocks, axis=0).reshape(-1)
    slot = jnp.where(listed >= 0, jnp.take(located, jnp.maximum(listed, 0)), -1)
    outs = []
    for sequence in range(sequences):
        heads = []
        for head in range(kv_heads):
            wide = slice(head * GROUP_WIDTH, (head + 1) * GROUP_WIDTH)
            narrow = slice(head * HEAD_SIZE, (head + 1) * HEAD_SIZE)
            kv = jnp.concatenate([key_home[sequence, :, narrow], value_home[sequence, :, narrow]], axis=1)
            kv = lax.all_gather(kv, "seq", axis=0, tiled=True)
            kv = kv.reshape(-1, BLOCK_TOKENS, 2 * HEAD_SIZE)
            q = query_home[sequence, :, wide].reshape(per_device, BLOCK_TOKENS, GROUP_WIDTH)
            g = grad_home[sequence, :, wide].reshape(per_device, BLOCK_TOKENS, GROUP_WIDTH)
            attention, query_grad, total = plain_attention(slot, q, g, kv, slots)
            total = lax.psum_scatter(total, "seq", scatter_dimension=0, tiled=True)
            total = total.astype(jnp.bfloat16).reshape(tokens, 2 * HEAD_SIZE)
            heads.append(
                (
                    attention.reshape(tokens, GROUP_WIDTH),
                    query_grad.reshape(tokens, GROUP_WIDTH),
                    total[:, :HEAD_SIZE],
                    total[:, HEAD_SIZE:],
                )
            )
        outs.append(tuple(jnp.concatenate(parts, axis=1) for parts in zip(*heads)))
    return tuple(jnp.stack(parts) for parts in zip(*outs))


def quad_kernel(listed_ref, position_ref, q_ref, g_ref, *refs, slots, lines, kv_heads, head):
    pieces, refs = refs[:3], refs[3:]
    kv_line, kv_beside, a_own, dq_own, far, total_line, total_beside = refs[:7]
    located, slot, q_at, g_at, kv_at, a_at, dq_at, total, keys_at, values_at, part, kv_sem, in_sem, out_sem = refs[7:]
    s = lax.axis_index("seq")
    h = lax.axis_index("head")
    x = (s >> 1) & 1
    half = lines * 4
    fetches = [
        pltpu.make_async_copy(ref, kv_at.at[pl.ds(n * half, half)], kv_sem.at[n])
        for n, ref in enumerate((kv_line, kv_beside))
    ]
    column = (h * 2 + x) * kv_heads + head
    span = pl.ds(pl.multiple_of(column * GROUP_WIDTH, GROUP_WIDTH), GROUP_WIDTH)
    for which, (ref, at) in enumerate(((q_ref, q_at), (g_ref, g_at))):
        fetches.append(pltpu.make_async_copy(ref.at[0, :, span], at.at[0], in_sem.at[which, 0]))
        for n in range(3):
            fetches.append(pltpu.make_async_copy(pieces[n].at[which], at.at[n + 1], in_sem.at[which, n + 1]))
    for fetch in fetches:
        fetch.start()

    def locate(j, carry):
        located[position_ref[j]] = j
        return carry

    lax.fori_loop(0, lines * 8, locate, 0)

    def entry(n, carry):
        i, e = n // slots, n % slots
        stored = ((s ^ (2 * (i >> 1))) * 2) + (h ^ (i & 1))
        b = listed_ref[position_ref[stored], e]
        home = located[jnp.maximum(b, 0)]
        seq_home = home >> 1
        where_ = ((seq_home ^ s) & 1) * half + (seq_home >> 2) * 4
        where_ = where_ + (((seq_home >> 1) & 1) ^ x) * 2 + ((home & 1) ^ h)
        slot[n] = jnp.where(b >= 0, where_, -1)
        return carry

    lax.fori_loop(0, 4 * slots, entry, 0)
    total[...] = jnp.zeros_like(total)
    for fetch in fetches:
        fetch.wait()

    def block(i, carry):
        attend_block(i, slot, q_at, g_at, kv_at, a_at, dq_at, total, keys_at, values_at, part, slots)
        row = pl.ds(pl.multiple_of((h ^ (i & 1)) * BLOCK_TOKENS, BLOCK_TOKENS), BLOCK_TOKENS)

        @pl.when(i < 2)
        def _():
            pltpu.make_async_copy(a_at.at[i], a_own.at[row], out_sem.at[0]).start()
            pltpu.make_async_copy(dq_at.at[i], dq_own.at[row], out_sem.at[1]).start()

        @pl.when(i >= 2)
        def _():
            pltpu.make_async_copy(a_at.at[i], far.at[0, row], out_sem.at[2]).start()
            pltpu.make_async_copy(dq_at.at[i], far.at[1, row], out_sem.at[2]).start()

        return carry

    lax.fori_loop(0, 4, block, 0)
    total_line[...] = total[:half].astype(jnp.bfloat16)
    total_beside[...] = total[half:].astype(jnp.bfloat16)
    for n, ref in enumerate((a_own, dq_own, far)):
        pltpu.make_async_copy(ref, ref, out_sem.at[n]).wait()


def quad_attention(kv_blocks, block_position, queries, output_gradient, pieces, kv_line, kv_beside, lines, kv_heads, head):
    outside = pl.BlockSpec(memory_space=pltpu.HBM)
    inside = pl.BlockSpec(memory_space=pltpu.VMEM)
    slots = kv_blocks.shape[1]
    half = lines * 4
    own = jax.ShapeDtypeStruct((2 * BLOCK_TOKENS, GROUP_WIDTH), jnp.bfloat16)
    sums = jax.ShapeDtypeStruct((half, BLOCK_TOKENS, 2 * HEAD_SIZE), jnp.bfloat16)
    wide = pltpu.VMEM((4, BLOCK_TOKENS, GROUP_WIDTH), jnp.bfloat16)
    return pl.pallas_call(
        functools.partial(quad_kernel, slots=slots, lines=lines, kv_heads=kv_heads, head=head),
        grid_spec=pltpu.PrefetchScalarGridSpec(
            num_scalar_prefetch=2,
            grid=(),
            in_specs=[outside] * 7,
            out_specs=[outside] * 3 + [inside] * 2,
            scratch_shapes=[
                pltpu.SMEM((lines * 8,), jnp.int32),
                pltpu.SMEM((4 * slots,), jnp.int32),
                wide,
                wide,
                pltpu.VMEM((2 * half, BLOCK_TOKENS, 2 * HEAD_SIZE), jnp.bfloat16),
                wide,
                wide,
                pltpu.VMEM((2 * half, BLOCK_TOKENS, 2 * HEAD_SIZE), jnp.float32),
                *scratch(slots),
                pltpu.SemaphoreType.DMA((2,)),
                pltpu.SemaphoreType.DMA((2, 4)),
                pltpu.SemaphoreType.DMA((3,)),
            ],
        ),
        out_shape=[own, own, jax.ShapeDtypeStruct((2, *own.shape), jnp.bfloat16), sums, sums],
        compiler_params=pltpu.CompilerParams(vmem_limit_bytes=60 << 20),
        cost_estimate=cost(4, slots, 2 * half, 2),
    )(kv_blocks, block_position, queries, output_gradient, *pieces, kv_line, kv_beside)


def pack_kernel(keys_ref, values_ref, *outs, kv_heads):
    h = lax.axis_index("head")
    x = (lax.axis_index("seq") >> 1) & 1
    for n, out in enumerate(outs):
        quarter = (h ^ (n & 1)) * 2 + (x ^ (n >> 1))
        for head in range(kv_heads):
            start = (quarter * kv_heads + head) * HEAD_SIZE
            span = pl.ds(pl.multiple_of(start, HEAD_SIZE), HEAD_SIZE)
            out[head, :, :HEAD_SIZE] = keys_ref[0, :, span]
            out[head, :, HEAD_SIZE:] = values_ref[0, :, span]


def pack(keys, values, kv_heads):
    inside = pl.BlockSpec(memory_space=pltpu.VMEM)
    shape = jax.ShapeDtypeStruct((kv_heads, BLOCK_TOKENS, 2 * HEAD_SIZE), jnp.bfloat16)
    return pl.pallas_call(
        functools.partial(pack_kernel, kv_heads=kv_heads),
        in_specs=[inside] * 2,
        out_specs=[inside] * 4,
        out_shape=[shape] * 4,
    )(keys, values)


def pack_wide_kernel(q_ref, g_ref, *refs, kv_heads, head):
    outs, (held, in_sem, out_sem) = refs[:3], refs[3:]
    h = lax.axis_index("head")
    x = (lax.axis_index("seq") >> 1) & 1
    fetches = []
    for n in range(3):
        quarter = (h ^ ((n + 1) & 1)) * 2 + (x ^ ((n + 1) >> 1))
        start = (quarter * kv_heads + head) * GROUP_WIDTH
        span = pl.ds(pl.multiple_of(start, GROUP_WIDTH), GROUP_WIDTH)
        for which, ref in enumerate((q_ref, g_ref)):
            fetches.append(pltpu.make_async_copy(ref.at[0, :, span], held.at[n, which], in_sem.at[n, which]))
    for fetch in fetches:
        fetch.start()
    stores = []
    for n in range(3):
        fetches[2 * n].wait()
        fetches[2 * n + 1].wait()
        stores.append(pltpu.make_async_copy(held.at[n], outs[n], out_sem.at[n]))
        stores[n].start()
    for store in stores:
        store.wait()


def pack_wide(queries, output_gradient, kv_heads, head):
    outside = pl.BlockSpec(memory_space=pltpu.HBM)
    shape = jax.ShapeDtypeStruct((2, BLOCK_TOKENS, GROUP_WIDTH), jnp.bfloat16)
    return pl.pallas_call(
        functools.partial(pack_wide_kernel, kv_heads=kv_heads, head=head),
        in_specs=[outside] * 2,
        out_specs=[outside] * 3,
        out_shape=[shape] * 3,
        scratch_shapes=[
            pltpu.VMEM((3, *shape.shape), jnp.bfloat16),
            pltpu.SemaphoreType.DMA((3, 2)),
            pltpu.SemaphoreType.DMA((3,)),
        ],
        cost_estimate=pl.CostEstimate(flops=0, transcendentals=0, bytes_accessed=12 * BLOCK_TOKENS * GROUP_WIDTH * 2),
    )(queries, output_gradient)


def spread_kernel(*refs, head):
    out = refs[-1]
    for line in range(out.shape[0] // 4):
        for n in range(4):
            out[line * 4 + n] = refs[n][head]


def spread(parts, head, lines):
    inside = pl.BlockSpec(memory_space=pltpu.VMEM)
    return pl.pallas_call(
        functools.partial(spread_kernel, head=head),
        in_specs=[inside] * 4,
        out_specs=inside,
        out_shape=jax.ShapeDtypeStruct((lines * 4, BLOCK_TOKENS, 2 * HEAD_SIZE), jnp.bfloat16),
    )(*parts)


def quad(queries, keys, values, output_gradient, kv_blocks, block_position):
    seq_count = lax.axis_size("seq")
    lines = seq_count // 4
    s = lax.axis_index("seq")
    h = lax.axis_index("head")
    x = (s // 2) % 2
    kv_heads = keys.shape[2] // HEAD_SIZE // 4
    across = [(0, 1), (1, 0)]
    beside = [(i, i ^ 1) for i in range(seq_count)]
    sideways = [(i, i ^ 2) for i in range(seq_count)]
    corner = [(i * 2 + j, (i ^ 2) * 2 + 1 - j) for i in range(seq_count) for j in range(2)]
    line_groups = [[line * 4 + r for line in range(lines)] for r in range(4)]

    def trade(parts):
        return [
            lax.ppermute(parts[0], "head", across),
            lax.ppermute(parts[1], "seq", sideways),
            lax.ppermute(parts[2], ("seq", "head"), corner),
        ]

    def along_line(array):
        return lax.all_to_all(array, "seq", split_axis=0, concat_axis=0, tiled=True, axis_index_groups=line_groups)

    own, *others = pack(keys, values, kv_heads)
    kv_parts = [own] + trade(others)
    pieces = []
    for head in range(kv_heads):
        parts = pack_wide(queries, output_gradient, kv_heads, head)
        pieces.append(trade(parts))
    kv_lines = []
    for head in range(kv_heads):
        copies = spread(kv_parts, head, lines)
        kv_lines.append(along_line(copies))
    own_parts = []
    far_parts = []
    grad_parts = []
    for head in range(kv_heads):
        kv_beside = lax.ppermute(kv_lines[head], "seq", beside)
        a_own, dq_own, far, total_line, total_beside = quad_attention(
            kv_blocks, block_position, queries, output_gradient, pieces[head], kv_lines[head], kv_beside, lines, kv_heads, head
        )
        arrived = lax.ppermute(total_beside, "seq", beside)
        far_parts.append(lax.ppermute(far, "seq", sideways))
        own_parts.append((a_own, dq_own))
        total = total_line.astype(jnp.float32) + arrived.astype(jnp.float32)
        returned = along_line(total.astype(jnp.bfloat16))
        returned = returned.reshape(lines, 2, 2, BLOCK_TOKENS, 2 * HEAD_SIZE)
        summed = jnp.sum(returned.astype(jnp.float32), axis=0).astype(jnp.bfloat16)
        grad_parts.append((summed[0], lax.ppermute(summed[1], "seq", sideways)))

    def place(own, far):
        return jnp.where(x == 0, jnp.concatenate(own + far, axis=-1), jnp.concatenate(far + own, axis=-1))

    outs = [place([part[n] for part in own_parts], [part[n] for part in far_parts])[None] for n in range(2)]
    for n in range(2):
        span = slice(n * HEAD_SIZE, (n + 1) * HEAD_SIZE)
        grad = place([part[0][..., span] for part in grad_parts], [part[1][..., span] for part in grad_parts])
        grad = jnp.where(h == 0, grad, grad[::-1])
        outs.append(grad.reshape(1, 2 * BLOCK_TOKENS, -1))
    return tuple(outs)


def body(queries, keys, values, output_gradient, kv_blocks, block_position):
    sequences, tokens, _ = queries.shape
    fits = (
        lax.axis_size("head") == 2
        and lax.axis_size("seq") % 4 == 0
        and sequences == 1
        and tokens == BLOCK_TOKENS
        and KEY_VALUE_HEADS % 4 == 0
    )
    chosen = quad if fits else general
    return chosen(queries, keys, values, output_gradient, kv_blocks, block_position)


def solution(mesh):
    placed = (
        P(None, ("seq", "head"), None),
        P(None, ("seq", "head"), None),
        P(None, ("seq", "head"), None),
        P(None, ("seq", "head"), None),
        P(),
        P(),
    )
    return jax.shard_map(
        body,
        mesh=mesh,
        in_specs=placed,
        out_specs=(
            P(None, "seq", "head"),
            P(None, "seq", "head"),
            P(None, "seq", "head"),
            P(None, "seq", "head"),
        ),
        check_vma=False,
    )
```

```python
import functools

import jax
import jax.numpy as jnp
from jax import lax
from jax.experimental import pallas as pl
from jax.experimental.pallas import tpu as pltpu
from jax.sharding import PartitionSpec as P


QUERY_HEADS = 64
KEY_VALUE_HEADS = 8
HEAD_SIZE = 128
BLOCK_TOKENS = 128
GROUP = QUERY_HEADS // KEY_VALUE_HEADS
GROUP_WIDTH = GROUP * HEAD_SIZE
LOG2E = 1.4426950408889634
FACTOR = HEAD_SIZE ** (-0.5)


NT = (((1,), (1,)), ((), ()))
TN = (((0,), (0,)), ((), ()))
NN = (((1,), (0,)), ((), ()))


def dot(a, b, dims):
    return lax.dot_general(a, b, dims, preferred_element_type=jnp.float32)


def held(*arrays):
    return [pltpu.with_memory_space_constraint(array, pltpu.HBM) for array in arrays]


def stored_index(block_position):
    block_list = block_position.shape[0]
    stored = jnp.arange(block_list, dtype=jnp.int32)
    matches = block_position[None, :] == stored[:, None]
    return jnp.sum(jnp.where(matches, stored[None, :], 0), axis=1)


def attend_block(i, slot_ref, q_ref, g_ref, kv_ref, a_ref, dq_ref, total, keys_at, values_at, slots):
    b = BLOCK_TOKENS
    d = HEAD_SIZE
    rows = GROUP * b
    at = [jnp.maximum(slot_ref[i * slots + e], 0) for e in range(slots)]
    bias = [jnp.where(slot_ref[i * slots + e] >= 0, 0.0, jnp.inf).astype(jnp.float32) for e in range(slots)]
    for e in range(slots):
        keys_at[e * b : (e + 1) * b, :] = kv_ref[at[e], :, :d]
        values_at[e * b : (e + 1) * b, :] = kv_ref[at[e], :, d:]
    spans = [slice(t * d, (t + 1) * d) for t in range(GROUP)]
    q = jnp.concatenate([q_ref[i, :, span] for span in spans], axis=0)
    g = jnp.concatenate([g_ref[i, :, span] for span in spans], axis=0)
    k = keys_at[...]
    v = values_at[...]
    s = dot(q, k, NT)
    column = lax.broadcasted_iota(jnp.int32, (rows, b), 1)
    row = lax.broadcasted_iota(jnp.int32, (rows, b), 0) & (b - 1)
    tiles = [jnp.where(column <= row, s[:, :b], -jnp.inf)]
    tiles += [s[:, e * b : (e + 1) * b] for e in range(1, slots)]
    high = tiles[0]
    for e in range(1, slots):
        high = jnp.maximum(high, tiles[e] - bias[e])
    high = jnp.max(high, axis=1, keepdims=True) * (FACTOR * LOG2E)
    powers = [jnp.exp2(tiles[e] * (FACTOR * LOG2E) - (high + bias[e])) for e in range(slots)]
    inverse = 1.0 / jnp.sum(functools.reduce(jnp.add, powers), axis=1, keepdims=True)
    probs = jnp.concatenate([power * inverse for power in powers], axis=1)
    probs_half = probs.astype(jnp.bfloat16)
    out = dot(probs_half, v, NN).astype(jnp.bfloat16)
    dprobs = dot(g, v, NT)
    delta = jnp.sum(g.astype(jnp.float32) * out.astype(jnp.float32), axis=1, keepdims=True)
    dscores = (probs * (dprobs - delta)).astype(jnp.bfloat16)
    dq = (dot(dscores, k, NN) * FACTOR).astype(jnp.bfloat16)
    for t, span in enumerate(spans):
        a_ref[i, :, span] = out[t * b : (t + 1) * b]
        dq_ref[i, :, span] = dq[t * b : (t + 1) * b]
    dk = dot(q, dscores, TN) * FACTOR
    dv = dot(g, probs_half, TN)
    for e in range(slots):
        span = slice(e * b, (e + 1) * b)
        total[at[e], :, :d] += jnp.transpose(dk[:, span])
        total[at[e], :, d:] += jnp.transpose(dv[:, span])


def cost(blocks, slots, stored, wide):
    return pl.CostEstimate(
        flops=10 * blocks * slots * GROUP * BLOCK_TOKENS * BLOCK_TOKENS * HEAD_SIZE,
        transcendentals=blocks * slots * GROUP * BLOCK_TOKENS * BLOCK_TOKENS,
        bytes_accessed=blocks * BLOCK_TOKENS * GROUP_WIDTH * 8
        + stored * BLOCK_TOKENS * 2 * HEAD_SIZE * (2 + wide),
    )


def scratch(slots):
    return [
        pltpu.VMEM((slots * BLOCK_TOKENS, HEAD_SIZE), jnp.bfloat16),
        pltpu.VMEM((slots * BLOCK_TOKENS, HEAD_SIZE), jnp.bfloat16),
    ]


def plain_kernel(slot_ref, q_ref, g_ref, kv_ref, a_ref, dq_ref, total, keys_at, values_at, *, slots):
    total[...] = jnp.zeros_like(total)

    def block(i, carry):
        attend_block(i, slot_ref, q_ref, g_ref, kv_ref, a_ref, dq_ref, total, keys_at, values_at, slots)
        return carry

    lax.fori_loop(0, q_ref.shape[0], block, 0)


def plain_attention(slot, q, g, kv, slots):
    whole = pl.BlockSpec(memory_space=pltpu.VMEM)
    like = jax.ShapeDtypeStruct(q.shape, jnp.bfloat16)
    return pl.pallas_call(
        functools.partial(plain_kernel, slots=slots),
        grid_spec=pltpu.PrefetchScalarGridSpec(
            num_scalar_prefetch=1,
            grid=(),
            in_specs=[whole] * 3,
            out_specs=[whole] * 3,
            scratch_shapes=scratch(slots),
        ),
        out_shape=[like, like, jax.ShapeDtypeStruct(kv.shape, jnp.float32)],
        compiler_params=pltpu.CompilerParams(vmem_limit_bytes=60 << 20),
        cost_estimate=cost(q.shape[0], slots, kv.shape[0], 4),
    )(slot, q, g, kv)


def general(queries, keys, values, output_gradient, kv_blocks, block_position):
    query_home, key_home, value_home, grad_home = (
        lax.all_to_all(a, "head", split_axis=2, concat_axis=1, tiled=True)
        for a in (queries, keys, values, output_gradient)
    )
    sequences, tokens, _ = query_home.shape
    kv_heads = key_home.shape[2] // HEAD_SIZE
    per_device = tokens // BLOCK_TOKENS
    slots = kv_blocks.shape[1]
    my_index = lax.axis_index("seq")
    located = stored_index(block_position)
    my_blocks = lax.dynamic_slice_in_dim(block_position, my_index * per_device, per_device)
    listed = jnp.take(kv_blocks, my_blocks, axis=0).reshape(-1)
    slot = jnp.where(listed >= 0, jnp.take(located, jnp.maximum(listed, 0)), -1)
    outs = []
    for sequence in range(sequences):
        heads = []
        for head in range(kv_heads):
            wide = slice(head * GROUP_WIDTH, (head + 1) * GROUP_WIDTH)
            narrow = slice(head * HEAD_SIZE, (head + 1) * HEAD_SIZE)
            kv = jnp.concatenate([key_home[sequence, :, narrow], value_home[sequence, :, narrow]], axis=1)
            kv = lax.all_gather(kv, "seq", axis=0, tiled=True)
            kv = kv.reshape(-1, BLOCK_TOKENS, 2 * HEAD_SIZE)
            q = query_home[sequence, :, wide].reshape(per_device, BLOCK_TOKENS, GROUP_WIDTH)
            g = grad_home[sequence, :, wide].reshape(per_device, BLOCK_TOKENS, GROUP_WIDTH)
            attention, query_grad, total = plain_attention(slot, q, g, kv, slots)
            total = lax.psum_scatter(total, "seq", scatter_dimension=0, tiled=True)
            total = total.astype(jnp.bfloat16).reshape(tokens, 2 * HEAD_SIZE)
            heads.append(
                (
                    attention.reshape(tokens, GROUP_WIDTH),
                    query_grad.reshape(tokens, GROUP_WIDTH),
                    total[:, :HEAD_SIZE],
                    total[:, HEAD_SIZE:],
                )
            )
        outs.append(tuple(jnp.concatenate(parts, axis=1) for parts in zip(*heads)))
    return tuple(jnp.stack(parts) for parts in zip(*outs))


def quad_kernel(listed_ref, position_ref, q_ref, g_ref, *refs, slots, lines, kv_heads, head):
    pieces, refs = refs[:3], refs[3:]
    kv_line, kv_beside, a_own, dq_own, far, total_line, total_beside = refs[:7]
    located, slot, q_at, g_at, kv_at, a_at, dq_at, total, keys_at, values_at, kv_sem, in_sem, out_sem = refs[7:]
    s = lax.axis_index("seq")
    h = lax.axis_index("head")
    x = (s >> 1) & 1
    half = lines * 4
    fetches = [
        pltpu.make_async_copy(ref, kv_at.at[pl.ds(n * half, half)], kv_sem.at[n])
        for n, ref in enumerate((kv_line, kv_beside))
    ]
    column = (h * 2 + x) * kv_heads + head
    span = pl.ds(pl.multiple_of(column * GROUP_WIDTH, GROUP_WIDTH), GROUP_WIDTH)
    for which, (ref, at) in enumerate(((q_ref, q_at), (g_ref, g_at))):
        fetches.append(pltpu.make_async_copy(ref.at[0, :, span], at.at[0], in_sem.at[which, 0]))
        for n in range(3):
            fetches.append(pltpu.make_async_copy(pieces[n].at[which], at.at[n + 1], in_sem.at[which, n + 1]))
    for fetch in fetches:
        fetch.start()

    def locate(j, carry):
        located[position_ref[j]] = j
        return carry

    lax.fori_loop(0, lines * 8, locate, 0)

    def entry(n, carry):
        i, e = n // slots, n % slots
        stored = ((s ^ (2 * (i >> 1))) * 2) + (h ^ (i & 1))
        b = listed_ref[e, position_ref[stored]]
        home = located[jnp.maximum(b, 0)]
        seq_home = home >> 1
        where_ = ((seq_home ^ s) & 1) * half + (seq_home >> 2) * 4
        where_ = where_ + (((seq_home >> 1) & 1) ^ x) * 2 + ((home & 1) ^ h)
        slot[n] = jnp.where(b >= 0, where_, -1)
        return carry

    lax.fori_loop(0, 4 * slots, entry, 0)
    total[...] = jnp.zeros_like(total)
    for fetch in fetches[:2]:
        fetch.wait()

    def block(i, carry):
        pltpu.make_async_copy(q_at.at[i], q_at.at[i], in_sem.at[0, i]).wait()
        pltpu.make_async_copy(g_at.at[i], g_at.at[i], in_sem.at[1, i]).wait()
        attend_block(i, slot, q_at, g_at, kv_at, a_at, dq_at, total, keys_at, values_at, slots)
        row = pl.ds(pl.multiple_of((h ^ (i & 1)) * BLOCK_TOKENS, BLOCK_TOKENS), BLOCK_TOKENS)

        @pl.when(i < 2)
        def _():
            pltpu.make_async_copy(a_at.at[i], a_own.at[row], out_sem.at[0]).start()
            pltpu.make_async_copy(dq_at.at[i], dq_own.at[row], out_sem.at[1]).start()

        @pl.when(i >= 2)
        def _():
            pltpu.make_async_copy(a_at.at[i], far.at[0, row], out_sem.at[2]).start()
            pltpu.make_async_copy(dq_at.at[i], far.at[1, row], out_sem.at[2]).start()

        return carry

    lax.fori_loop(0, 4, block, 0)
    total_line[...] = total[:half].astype(jnp.bfloat16)
    total_beside[...] = total[half:].astype(jnp.bfloat16)
    for n, ref in enumerate((a_own, dq_own, far)):
        pltpu.make_async_copy(ref, ref, out_sem.at[n]).wait()


def quad_attention(kv_blocks, block_position, queries, output_gradient, pieces, kv_line, kv_beside, lines, kv_heads, head):
    outside = pl.BlockSpec(memory_space=pl.ANY)
    inside = pl.BlockSpec(memory_space=pltpu.VMEM)
    slots = kv_blocks.shape[1]
    half = lines * 4
    own = pltpu.HBM((2 * BLOCK_TOKENS, GROUP_WIDTH), jnp.bfloat16)
    sums = pltpu.HBM((half, BLOCK_TOKENS, 2 * HEAD_SIZE), jnp.bfloat16)
    wide = pltpu.VMEM((4, BLOCK_TOKENS, GROUP_WIDTH), jnp.bfloat16)
    return pl.pallas_call(
        functools.partial(quad_kernel, slots=slots, lines=lines, kv_heads=kv_heads, head=head),
        grid_spec=pltpu.PrefetchScalarGridSpec(
            num_scalar_prefetch=2,
            grid=(),
            in_specs=[outside] * 7,
            out_specs=[outside] * 3 + [inside] * 2,
            scratch_shapes=[
                pltpu.SMEM((lines * 8,), jnp.int32),
                pltpu.SMEM((4 * slots,), jnp.int32),
                wide,
                wide,
                pltpu.VMEM((2 * half, BLOCK_TOKENS, 2 * HEAD_SIZE), jnp.bfloat16),
                wide,
                wide,
                pltpu.VMEM((2 * half, BLOCK_TOKENS, 2 * HEAD_SIZE), jnp.float32),
                *scratch(slots),
                pltpu.SemaphoreType.DMA((2,)),
                pltpu.SemaphoreType.DMA((2, 4)),
                pltpu.SemaphoreType.DMA((3,)),
            ],
        ),
        out_shape=[own, own, pltpu.HBM((2, 2 * BLOCK_TOKENS, GROUP_WIDTH), jnp.bfloat16), sums, sums],
        compiler_params=pltpu.CompilerParams(vmem_limit_bytes=44 << 20),
        cost_estimate=cost(4, slots, 2 * half, 2),
    )(jnp.transpose(kv_blocks), block_position, *held(queries, output_gradient), *pieces, kv_line, kv_beside)


def pack_kernel(keys_ref, values_ref, *outs, kv_heads):
    h = lax.axis_index("head")
    x = (lax.axis_index("seq") >> 1) & 1
    for n, out in enumerate(outs):
        quarter = (h ^ (n & 1)) * 2 + (x ^ (n >> 1))
        for head in range(kv_heads):
            start = (quarter * kv_heads + head) * HEAD_SIZE
            span = pl.ds(pl.multiple_of(start, HEAD_SIZE), HEAD_SIZE)
            out[head, :, :HEAD_SIZE] = keys_ref[0, :, span]
            out[head, :, HEAD_SIZE:] = values_ref[0, :, span]


def pack(keys, values, kv_heads):
    inside = pl.BlockSpec(memory_space=pltpu.VMEM)
    shape = pltpu.HBM((kv_heads, BLOCK_TOKENS, 2 * HEAD_SIZE), jnp.bfloat16)
    return pl.pallas_call(
        functools.partial(pack_kernel, kv_heads=kv_heads),
        in_specs=[inside] * 2,
        out_specs=[inside] * 4,
        out_shape=[shape] * 4,
    )(*held(keys, values))


def pack_wide_kernel(q_ref, g_ref, *refs, kv_heads, head):
    outs, (held, in_sem, out_sem) = refs[:3], refs[3:]
    h = lax.axis_index("head")
    x = (lax.axis_index("seq") >> 1) & 1
    fetches = []
    for n in range(3):
        quarter = (h ^ ((n + 1) & 1)) * 2 + (x ^ ((n + 1) >> 1))
        start = (quarter * kv_heads + head) * GROUP_WIDTH
        span = pl.ds(pl.multiple_of(start, GROUP_WIDTH), GROUP_WIDTH)
        for which, ref in enumerate((q_ref, g_ref)):
            fetches.append(pltpu.make_async_copy(ref.at[0, :, span], held.at[n, which], in_sem.at[n, which]))
    for fetch in fetches:
        fetch.start()
    stores = []
    for n in range(3):
        fetches[2 * n].wait()
        fetches[2 * n + 1].wait()
        stores.append(pltpu.make_async_copy(held.at[n], outs[n], out_sem.at[n]))
        stores[n].start()
    for store in stores:
        store.wait()


def pack_wide(queries, output_gradient, kv_heads, head):
    outside = pl.BlockSpec(memory_space=pltpu.HBM)
    shape = pltpu.HBM((2, BLOCK_TOKENS, GROUP_WIDTH), jnp.bfloat16)
    return pl.pallas_call(
        functools.partial(pack_wide_kernel, kv_heads=kv_heads, head=head),
        in_specs=[outside] * 2,
        out_specs=[outside] * 3,
        out_shape=[shape] * 3,
        scratch_shapes=[
            pltpu.VMEM((3, 2, BLOCK_TOKENS, GROUP_WIDTH), jnp.bfloat16),
            pltpu.SemaphoreType.DMA((3, 2)),
            pltpu.SemaphoreType.DMA((3,)),
        ],
        cost_estimate=pl.CostEstimate(flops=0, transcendentals=0, bytes_accessed=12 * BLOCK_TOKENS * GROUP_WIDTH * 2),
    )(*held(queries, output_gradient))


def spread_kernel(*refs, head):
    parts, (out, at, in_sem, out_sem) = refs[:4], refs[4:]
    fetches = [pltpu.make_async_copy(part.at[head], at.at[n], in_sem.at[n]) for n, part in enumerate(parts)]
    for fetch in fetches:
        fetch.start()
    for fetch in fetches:
        fetch.wait()
    stores = [
        pltpu.make_async_copy(at, out.at[pl.ds(line * 4, 4)], out_sem.at[line]) for line in range(out.shape[0] // 4)
    ]
    for store in stores:
        store.start()
    for store in stores:
        store.wait()


def spread(parts, head, lines):
    anywhere = pl.BlockSpec(memory_space=pl.ANY)
    return pl.pallas_call(
        functools.partial(spread_kernel, head=head),
        in_specs=[anywhere] * 4,
        out_specs=anywhere,
        out_shape=pltpu.HBM((lines * 4, BLOCK_TOKENS, 2 * HEAD_SIZE), jnp.bfloat16),
        scratch_shapes=[
            pltpu.VMEM((4, BLOCK_TOKENS, 2 * HEAD_SIZE), jnp.bfloat16),
            pltpu.SemaphoreType.DMA((4,)),
            pltpu.SemaphoreType.DMA((lines,)),
        ],
        compiler_params=pltpu.CompilerParams(vmem_limit_bytes=8 << 20),
    )(*parts)


def merge_kernel(a_ref, b_ref, out_ref, at, out_at, in_sem, out_sem, *, lines):
    fetches = [
        [pltpu.make_async_copy(ref.at[pl.ds(n * 4, 4)], at.at[m, n], in_sem.at[m, n]) for m, ref in enumerate((a_ref, b_ref))]
        for n in range(lines)
    ]
    for pair in fetches:
        for fetch in pair:
            fetch.start()
    stores = []
    for n in range(lines):
        for fetch in fetches[n]:
            fetch.wait()
        out_at[n] = (at[0, n].astype(jnp.float32) + at[1, n].astype(jnp.float32)).astype(jnp.bfloat16)
        stores.append(pltpu.make_async_copy(out_at.at[n], out_ref.at[pl.ds(n * 4, 4)], out_sem.at[n]))
        stores[n].start()
    for store in stores:
        store.wait()


def merge(a, b, lines):
    anywhere = pl.BlockSpec(memory_space=pl.ANY)
    piece = (4, *a.shape[1:])
    return pl.pallas_call(
        functools.partial(merge_kernel, lines=lines),
        in_specs=[anywhere] * 2,
        out_specs=anywhere,
        out_shape=pltpu.HBM(a.shape, jnp.bfloat16),
        scratch_shapes=[
            pltpu.VMEM((2, lines, *piece), jnp.bfloat16),
            pltpu.VMEM((lines, *piece), jnp.bfloat16),
            pltpu.SemaphoreType.DMA((2, lines)),
            pltpu.SemaphoreType.DMA((lines,)),
        ],
        compiler_params=pltpu.CompilerParams(vmem_limit_bytes=16 << 20),
    )(a, b)


def quad(queries, keys, values, output_gradient, kv_blocks, block_position):
    seq_count = lax.axis_size("seq")
    lines = seq_count // 4
    s = lax.axis_index("seq")
    h = lax.axis_index("head")
    x = (s // 2) % 2
    kv_heads = keys.shape[2] // HEAD_SIZE // 4
    across = [(0, 1), (1, 0)]
    beside = [(i, i ^ 1) for i in range(seq_count)]
    sideways = [(i, i ^ 2) for i in range(seq_count)]
    corner = [(i * 2 + j, (i ^ 2) * 2 + 1 - j) for i in range(seq_count) for j in range(2)]
    line_groups = [[line * 4 + r for line in range(lines)] for r in range(4)]

    def trade(parts):
        return [
            lax.ppermute(parts[0], "head", across),
            lax.ppermute(parts[1], "seq", sideways),
            lax.ppermute(parts[2], ("seq", "head"), corner),
        ]

    def along_line(array):
        return lax.all_to_all(array, "seq", split_axis=0, concat_axis=0, tiled=True, axis_index_groups=line_groups)

    own, *others = pack(keys, values, kv_heads)
    kv_parts = [own] + trade(others)
    pieces = []
    for head in range(kv_heads):
        parts = pack_wide(queries, output_gradient, kv_heads, head)
        pieces.append(trade(parts))
    kv_lines = []
    for head in range(kv_heads):
        copies = spread(kv_parts, head, lines)
        kv_lines.append(along_line(copies))
    own_parts = []
    far_parts = []
    grad_parts = []
    for head in range(kv_heads):
        kv_beside = lax.ppermute(kv_lines[head], "seq", beside)
        a_own, dq_own, far, total_line, total_beside = quad_attention(
            kv_blocks, block_position, queries, output_gradient, pieces[head], kv_lines[head], kv_beside, lines, kv_heads, head
        )
        arrived = lax.ppermute(total_beside, "seq", beside)
        far_parts.append(lax.ppermute(far, "seq", sideways))
        own_parts.append((a_own, dq_own))
        total = merge(total_line, arrived, lines)
        returned = along_line(total)
        returned = returned.reshape(lines, 2, 2, BLOCK_TOKENS, 2 * HEAD_SIZE)
        summed = jnp.sum(returned.astype(jnp.float32), axis=0).astype(jnp.bfloat16)
        grad_parts.append((summed[0], lax.ppermute(summed[1], "seq", sideways)))

    def place(own, far):
        return jnp.where(x == 0, jnp.concatenate(own + far, axis=-1), jnp.concatenate(far + own, axis=-1))

    outs = [place([part[n] for part in own_parts], [part[n] for part in far_parts])[None] for n in range(2)]
    for n in range(2):
        span = slice(n * HEAD_SIZE, (n + 1) * HEAD_SIZE)
        grad = place([part[0][..., span] for part in grad_parts], [part[1][..., span] for part in grad_parts])
        grad = jnp.where(h == 0, grad, grad[::-1])
        outs.append(grad.reshape(1, 2 * BLOCK_TOKENS, -1))
    return tuple(outs)


def body(queries, keys, values, output_gradient, kv_blocks, block_position):
    sequences, tokens, _ = queries.shape
    fits = (
        lax.axis_size("head") == 2
        and lax.axis_size("seq") % 4 == 0
        and sequences == 1
        and tokens == BLOCK_TOKENS
        and KEY_VALUE_HEADS % 4 == 0
    )
    chosen = quad if fits else general
    return chosen(queries, keys, values, output_gradient, kv_blocks, block_position)


def solution(mesh):
    placed = (
        P(None, ("seq", "head"), None),
        P(None, ("seq", "head"), None),
        P(None, ("seq", "head"), None),
        P(None, ("seq", "head"), None),
        P(),
        P(),
    )
    return jax.shard_map(
        body,
        mesh=mesh,
        in_specs=placed,
        out_specs=(
            P(None, "seq", "head"),
            P(None, "seq", "head"),
            P(None, "seq", "head"),
            P(None, "seq", "head"),
        ),
        check_vma=False,
    )
```
